256 devices in a mesh: dom: 64 (over x, z, core), rep: 4 (over y).
Axes of the slice: x: 4, y: 4, z: 8, core: 2. Of those that a mesh axis runs over, the one named last changes fastest.
Arguments:
- spline_blocks: bfloat16 [2048, 2, 64, 128], P(('dom', 'rep')), may hold values from -0.75 to 0.75
- modal_coeff: bfloat16 [64, 2, 8], replicated, may hold values from -6 to 6
- frequency: float32 [8], replicated, may hold values from 0.2 to 0.8
- face_dest: int32 [262144, 1], P('dom'), may hold values from 0 to 63; in each aligned block of 4096 rows (0 to 4095, 4096 to 8191, ...) at most 128 rows name the same one
- face_cell: int32 [262144], P('dom'), may hold values from 0 to 2047
- wall_weight: float32 [5, 2, 131072], P(None, None, 'dom'), may hold values from -6 to 6
- flow_rhs: float32 [5, 2, 8, 131072], P(None, None, 'rep', 'dom'), may hold values from -6 to 6
- previous: float32 [5, 2, 8, 131072], P(None, None, 'rep', 'dom'), may hold values from -6 to 6
- diag_inverse: float32 [5, 5, 131072], P(None, None, 'dom'), may hold values from -0.3 to 1.2
- off_jacobian: bfloat16 [6, 5, 5, 131072], P(None, None, None, 'dom'), may hold values from -0.5 to 0.5
- neighbor: int32 [6, 131072], P(None, 'dom'), may hold values from 0 to 3071, as said below
- send_list: int32 [4, 16384], P(None, 'dom'), may hold values from 0 to 2047
Outputs:
- solution: float32 [5, 2, 8, 131072], P(None, None, 'rep', 'dom')
The draws below stay inside these ranges and needn't reach their ends.
Inputs may be any that keep to these rules, and one draw needn't show every extreme that they name: `face_dest`: in each aligned block of 4096 rows (the rows of one index of dom), no partition is named by more than 128 rows, and in every draw some partition is named by exactly 128 rows of some block. `neighbor`: entries below 2048 name a cell of the same partition; entry 2048 + k * 256 + i names ghost row i of block k.
All inputs are finite; a program needn't handle non-finite values.
Results may differ from the reference program's by a relative error of at most 0.0003.
Values may be sent and summed in bfloat16 or wider, within the bound.
No kernel may reach another device: no remote copies, remote signals or barrier semaphores. Data moves between devices by JAX's collectives and lax.ppermute only.
A program may use at most 64 MiB of HBM per device.

```python
import math
import jax
import jax.numpy as jnp
import numpy as np
from jax import lax

MODES = 64
PAIRS = 8
SWEEPS = 2
CELLS = 2048
HALO = 256
FACE_DOM = 4096
CAP = 128
NFACES = 262144
NBLK = 2048
NCELLS = 131072
NSEND = 16384
N_DOM = 64


def draw_diag_inverse(key, part):
    first_key, second_key = jax.random.split(jax.random.fold_in(key, 11))
    diagonal_part = jnp.minimum(jnp.exp(jax.random.uniform(first_key, (5, 5, NCELLS), jnp.float32, math.log(0.4), math.log(1.3))), 1.2)
    other_part = jnp.clip(0.15 * jax.random.normal(second_key, (5, 5, NCELLS), jnp.float32), -0.3, 0.3)
    identity = jnp.eye(5, dtype=jnp.float32)[:, :, None]
    return jnp.where(identity > 0.5, diagonal_part, other_part).astype(jnp.float32)


def draw_neighbor(key, part):
    pick_key, local_key, ghost_key = jax.random.split(jax.random.fold_in(key, 23), 3)
    chooser = jax.random.randint(pick_key, (6, NCELLS), 0, 8)
    local_rows = jax.random.randint(local_key, (6, NCELLS), 0, CELLS)
    ghost_rows = jax.random.randint(ghost_key, (6, NCELLS), CELLS, CELLS + 4 * HALO)
    return jnp.where(chooser == 0, ghost_rows, local_rows).astype(jnp.int32)


def with_ends(array, key, least, largest):
    shape = array.shape
    index_at = [jax.random.randint(jax.random.fold_in(key, axis), (), 0, shape[axis]) for axis in range(len(shape))]
    array = array.at[tuple(index_at)].set(least)
    longest = shape.index(max(shape))
    index_at[longest] = (index_at[longest] + 1) % shape[longest]
    return array.at[tuple(index_at)].set(largest)


def level_of(key, dims, shards, smallest, largest):
    gain = 1.0
    for axis_at, blocks in shards:
        steps = jax.random.uniform(jax.random.fold_in(jax.random.fold_in(key, 6), axis_at), (blocks,), jnp.float32, smallest / len(shards), largest / len(shards))
        gain = gain * jnp.repeat(jnp.exp(steps), dims[axis_at] // blocks).reshape((-1,) + (1,) * (len(dims) - 1 - axis_at))
    return gain


def assign_block(own_key, own, number, rows, amount, top, reach, slope):
    sequence = jax.random.permutation(own_key, amount)
    packed, ordinary = portions_of(amount, rows * top, reach, slope, True), portions_of(amount, rows * top, reach, slope, False)
    places = jnp.arange(amount)

    def named(lengths, turn):
        used = int((lengths > 0).sum())
        fixed = max(1, used // 4)
        shifted = fixed + (places - fixed + turn * (used - fixed)) % max(1, amount - fixed)
        return jnp.zeros((amount,), jnp.int32).at[sequence[jnp.where(places < fixed, places, shifted)]].set(jnp.asarray(lengths, jnp.int32))

    lengths = jnp.where(number % 4 == 0, named(packed, number // 4), named(ordinary, number - number // 4 - 1))
    mixed = jax.random.permutation(jax.random.fold_in(own, 3), amount)
    source_of, receiver = mixed[0:amount // 2 * 2:2], mixed[1:amount // 2 * 2:2]
    margin = jnp.minimum(lengths[source_of] - 1, reach - lengths[receiver]) // 2
    margin = jnp.where((source_of == sequence[0]) | (receiver == sequence[0]) | (lengths[receiver] == 0), 0, jnp.maximum(margin, 0))
    shifted = jax.random.randint(jax.random.fold_in(own, 4), (amount // 2,), 0, 1 << 20) % (margin + 1)
    lengths = lengths.at[source_of].add(-shifted).at[receiver].add(shifted)
    items = jnp.searchsorted(jnp.cumsum(lengths), jnp.arange(rows * top), side="right").astype(jnp.int32)
    listing = items.reshape(top, rows).T
    listing = listing[jax.random.permutation(jax.random.fold_in(own, 1), rows)]
    turn = jax.random.randint(jax.random.fold_in(own, 2), (rows, 1), 0, top)
    return jnp.take_along_axis(listing, (jnp.arange(top)[None, :] + turn) % top, axis=1)


def portions_of(amount, total, limit, lean, full):
    portions = [(1 << 20) // math.isqrt(rank ** lean) + 1 for rank in range(1, amount + 1)]
    largest = limit if full else min(limit, max(-(-total // amount), total * portions[0] // sum(portions)))
    least = 1 if total - largest >= amount - 1 else 0
    holding, spare = [largest] + [least] * (amount - 1), total - largest - least * (amount - 1)
    while spare > 0:
        movable = [i for i in range(1, amount) if holding[i] < largest] or [i for i in range(1, amount) if holding[i] < limit]
        mass, left = sum([portions[i] for i in movable]), spare
        for i in movable:
            more = min(limit - holding[i], max(1, left * portions[i] // mass), spare)
            holding[i] = holding[i] + more
            spare = spare - more
    return np.array(holding)


def noise(key, dims, width, bound, cuts=(), kind=jnp.bfloat16):
    factor_of = level_of(key, dims, cuts, -0.22, 0.18) if cuts else 1.0
    array = jax.random.normal(key, dims, jnp.float32) * width * factor_of
    return jnp.minimum(jnp.maximum(array, -bound), bound).astype(kind)


def setup_inputs(seed: int = 0) -> dict:
    streams_of = jax.random.split(jax.random.key(seed), 13)
    spline_blocks = noise(streams_of[0], (NBLK, 2, MODES, 128), MODES ** -0.5, 0.75, ((0, 256),))
    modal_coeff = noise(streams_of[1], (MODES, 2, PAIRS), 1.0, 6.0)
    frequency = jnp.clip(jnp.exp(jax.random.uniform(streams_of[2], (PAIRS,), jnp.float32, math.log(0.2), math.log(0.8))), 0.2, 0.8)
    face_dest_keys = jax.random.split(jax.random.fold_in(streams_of[3], 1), NFACES // FACE_DOM)
    face_dest_turns = jax.random.permutation(jax.random.fold_in(streams_of[3], 3), NFACES // FACE_DOM)
    face_dest = jax.vmap(lambda own, number: assign_block(jax.random.fold_in(streams_of[3], 2), own, number, FACE_DOM, N_DOM, 1, CAP, 2))(face_dest_keys, face_dest_turns).reshape((NFACES, 1))
    face_cell = with_ends(jax.random.randint(streams_of[4], (NFACES,), 0, CELLS), jax.random.fold_in(streams_of[4], 1), 0, CELLS - 1).astype(jnp.int32)
    wall_weight = noise(streams_of[5], (5, 2, NCELLS), 1.0, 6.0, ((2, 64),), jnp.float32)
    flow_rhs = noise(streams_of[6], (5, 2, PAIRS, NCELLS), 1.0, 6.0, ((2, 4), (3, 64)), jnp.float32)
    previous = noise(streams_of[7], (5, 2, PAIRS, NCELLS), 1.0, 6.0, ((2, 4), (3, 64)), jnp.float32)
    diag_inverse = draw_diag_inverse(jax.random.fold_in(streams_of[12], 71), 0)
    off_jacobian = noise(streams_of[9], (6, 5, 5, NCELLS), 0.08, 0.5, ((3, 64),))
    neighbor = draw_neighbor(jax.random.fold_in(streams_of[12], 71), 0)
    send_list = with_ends(jax.random.randint(streams_of[11], (4, NSEND), 0, CELLS), jax.random.fold_in(streams_of[11], 1), 0, CELLS - 1).astype(jnp.int32)
    return {"spline_blocks": spline_blocks, "modal_coeff": modal_coeff, "frequency": frequency, "face_dest": face_dest, "face_cell": face_cell, "wall_weight": wall_weight, "flow_rhs": flow_rhs, "previous": previous, "diag_inverse": diag_inverse, "off_jacobian": off_jacobian, "neighbor": neighbor, "send_list": send_list}


offsets = (1, -1, 2, -2)


def face_values(blocks_in, coeff_in, freq_in):
    mode_count = coeff_in.shape[0]
    column_count = coeff_in.shape[2]
    flat_coeff = coeff_in.astype(jnp.float32).reshape(mode_count, 2 * column_count)
    products = jnp.einsum("kqmr,mz->qzkr", blocks_in.astype(jnp.float32), flat_coeff, precision=lax.Precision.HIGHEST)
    products = products.reshape(2, 2, column_count, blocks_in.shape[0] * blocks_in.shape[3])
    angular = freq_in[:, None]
    velocity = jnp.stack([-angular * products[0, 1], angular * products[0, 0]])
    return jnp.stack([velocity, products[1]])


def reference(spline_blocks, modal_coeff, frequency, face_dest, face_cell, wall_weight, flow_rhs, previous, diag_inverse, off_jacobian, neighbor, send_list):
    face_data = face_values(spline_blocks, modal_coeff, frequency)
    target = (face_dest[:, 0] * CELLS + face_cell).astype(jnp.int32)
    wall_sum = jnp.zeros((2, 2, PAIRS, NCELLS), jnp.float32).at[:, :, :, target].add(face_data)
    rhs_full = flow_rhs + wall_weight[:, 0, None, None, :] * wall_sum[0][None] + wall_weight[:, 1, None, None, :] * wall_sum[1][None]
    send_rows = send_list.reshape(4, N_DOM, HALO)
    local_index = neighbor.reshape(6, N_DOM, CELLS)
    angular = frequency[None, :, None]
    iterate = previous
    for sweep_index in range(SWEEPS):
        parted = iterate.reshape(5, 2, PAIRS, N_DOM, CELLS)
        ghost_list = []
        for slot_index in range(4):
            picked = jnp.take_along_axis(parted, send_rows[slot_index][None, None, None], axis=4)
            ghost_list.append(jnp.roll(picked, offsets[slot_index], axis=3))
        extended = jnp.concatenate([parted] + ghost_list, axis=4)
        coupling = jnp.zeros((5, 2, PAIRS, NCELLS), jnp.float32)
        for face_index in range(6):
            beside = jnp.take_along_axis(extended, local_index[face_index][None, None, None], axis=4).reshape(5, 2, PAIRS, NCELLS)
            jacobian = off_jacobian[face_index].astype(jnp.float32)
            for comp_index in range(5):
                coupling = coupling + jacobian[:, comp_index, None, None, :] * beside[comp_index][None]
        spinning = jnp.stack([-angular * iterate[:, 1], angular * iterate[:, 0]], axis=1)
        residual_now = rhs_full - coupling - spinning
        update = jnp.zeros((5, 2, PAIRS, NCELLS), jnp.float32)
        for comp_index in range(5):
            update = update + diag_inverse[:, comp_index, None, None, :] * residual_now[comp_index][None]
        iterate = update
    return iterate
```

```python
import jax
import jax.numpy as jnp
from jax import lax
from jax.experimental import pallas as pl
from jax.experimental.pallas import tpu as pltpu
from jax.sharding import PartitionSpec as P

SWEEPS = 2
F32 = jnp.float32
BF16 = jnp.bfloat16
LANES = 128
NT = (((1,), (1,)), ((), ()))


def from_behind(value, axis, by):
    length = lax.axis_size(axis)
    return lax.ppermute(value, axis, [(i, (i + by) % length) for i in range(length)])


def kernel_call(body, outs, scratch=()):
    return pl.pallas_call(
        body,
        out_shape=[jax.ShapeDtypeStruct(shape, dtype) for shape, dtype in outs],
        scratch_shapes=list(scratch),
        compiler_params=pltpu.CompilerParams(vmem_limit_bytes=56 << 20),
    )


def bcast(ref, row, rows=8):
    return ref[pl.ds(row, rows, stride=0), :]


def face_kernel(coef_ref, spline_ref, out_ref):
    coef = coef_ref[...]
    blocks = spline_ref.shape[0]
    for k in range(blocks):
        for q in range(2):
            v = jnp.dot(coef, spline_ref[k, q], preferred_element_type=F32)
            for y in range(4):
                out_ref[y, q * 4 : q * 4 + 4, k * LANES : (k + 1) * LANES] = v[y * 4 : y * 4 + 4]


def dispatch_kernel(vals_ref, dest_ref, cell_ref, out_ref, o_ref, a_ref, b_ref):
    doms = out_ref.shape[0] // 9
    tiles = dest_ref.shape[0]
    iota_d = lax.broadcasted_iota(jnp.int32, (doms, LANES), 0)
    iota_p = lax.broadcasted_iota(jnp.int32, (LANES, LANES), 0)
    iota_l = lax.broadcasted_iota(jnp.int32, (LANES, LANES), 1)
    upper = jnp.concatenate(
        [jnp.where(iota_p <= iota_l, 1.0, 0.0), jnp.ones((LANES, LANES), F32)], axis=1
    ).astype(BF16)
    for t in range(tiles):
        o_ref[t * doms : (t + 1) * doms, :] = jnp.where(
            iota_d == bcast(dest_ref, t, doms), 1.0, 0.0
        ).astype(BF16)
    carry = jnp.zeros((doms, LANES), F32)
    per_rep = tiles // 4
    for t in range(tiles):
        one = o_ref[t * doms : (t + 1) * doms, :]
        counts = jnp.dot(one, upper, preferred_element_type=F32)
        place = counts[:, :LANES] + carry
        carry = carry + counts[:, LANES:]
        pos = jnp.sum(one.astype(F32) * place, axis=0, keepdims=True).astype(jnp.int32) - 1
        lanes = slice(t * LANES, (t + 1) * LANES)
        b_ref[:, lanes] = jnp.where(iota_p == pos, 1.0, 0.0).astype(BF16)
        part = slice((t % per_rep) * LANES, (t % per_rep + 1) * LANES)
        v8 = vals_ref[t // per_rep, :, part]
        hi8 = v8.astype(BF16).astype(F32)
        lo8 = v8 - hi8
        for v in range(8):
            hi = jnp.broadcast_to(hi8[v : v + 1], (doms, LANES)).astype(BF16)
            lo = jnp.broadcast_to(lo8[v : v + 1], (doms, LANES)).astype(BF16)
            a_ref[v * doms : (v + 1) * doms, lanes] = hi * one
            a_ref[(9 + v) * doms : (10 + v) * doms, lanes] = lo * one
        cell = bcast(cell_ref, t, doms)
        a_ref[8 * doms : 9 * doms, lanes] = ((cell >> 7) << 7).astype(F32).astype(BF16) * one
        a_ref[17 * doms : 18 * doms, lanes] = (cell & 127).astype(F32).astype(BF16) * one
    acc = lax.dot_general(a_ref[...], b_ref[...], NT, preferred_element_type=F32)
    for v in range(9):
        out_ref[pl.ds(v, doms, stride=9), :] = (
            acc[v * doms : (v + 1) * doms] + acc[(9 + v) * doms : (10 + v) * doms]
        )


def field_row(f, t):
    return (f // 2) * 32 + t * 2 + f % 2


def load_half(ref, f, h):
    return ref[pl.ds(field_row(f, 8 * h), 8, stride=2), :]


def store_half(ref, f, h, value):
    ref[pl.ds(field_row(f, 8 * h), 8, stride=2), :] = value


def lane_take(row, lanes):
    return jnp.take_along_axis(row, lanes, axis=1, mode="promise_in_bounds")


def pick_rows(src_ref, send_ref, out_refs):
    idx = send_ref[...]
    hi, lo = idx >> 7, idx & 127
    masks = [hi == t for t in range(16)]
    for f in range(20):
        acc = lane_take(bcast(src_ref, field_row(f, 0)), lo)
        for t in range(1, 16):
            acc = jnp.where(masks[t], lane_take(bcast(src_ref, field_row(f, t)), lo), acc)
        for k in range(4):
            out_refs[k][f * 2 : f * 2 + 2, :] = acc[2 * k : 2 * k + 2]


def pick_kernel(src_ref, send_ref, *out_refs):
    pick_rows(src_ref, send_ref, out_refs)


def couple(h, src_ref, ghost_refs, near_ref, jac_ref):
    coupling = [None] * 20
    for j in range(6):
        idx = near_ref[j * 16 + h * 8 : j * 16 + h * 8 + 8, :]
        hi, lo = idx >> 7, idx & 127
        masks = [hi == t for t in range(24)]
        for g in range(5):
            beside = []
            for rp in range(4):
                f = g * 4 + rp
                acc = lane_take(bcast(src_ref, field_row(f, 0)), lo)
                for t in range(1, 16):
                    acc = jnp.where(masks[t], lane_take(bcast(src_ref, field_row(f, t)), lo), acc)
                for t in range(8):
                    row = bcast(ghost_refs[t // 2], f * 2 + t % 2)
                    acc = jnp.where(masks[16 + t], lane_take(row, lo), acc)
                beside.append(acc)
            for e in range(5):
                row = ((j * 5 + e) * 5 + g) * 16 + h * 8
                jac = jac_ref[row : row + 8, :]
                for rp in range(4):
                    term = jac * beside[rp]
                    at = e * 4 + rp
                    coupling[at] = term if coupling[at] is None else coupling[at] + term
    return coupling


def add_spin(h, coupling, src_ref, freq):
    for g in range(5):
        for p in range(2):
            re, im = g * 4 + p, g * 4 + 2 + p
            coupling[re] = coupling[re] - freq[p] * load_half(src_ref, im, h)
            coupling[im] = coupling[im] + freq[p] * load_half(src_ref, re, h)


def own_freq(freq_ref):
    first = lax.axis_index("rep") * 2
    return [freq_ref[first], freq_ref[first + 1]]


def solve(h, diag_ref, e, rp, parts):
    total = None
    for g in range(5):
        row = (e * 5 + g) * 16 + h * 8
        term = diag_ref[row : row + 8, :] * parts[g * 4 + rp]
        total = term if total is None else total + term
    return total


def first_kernel(freq_ref, src_ref, g0, g1, g2, g3, near_ref, jac_ref, diag_ref, flow_ref, weight_ref, pre_ref, base_ref, map_ref):
    freq = own_freq(freq_ref)
    for h in range(2):
        flow = [load_half(flow_ref, f, h) for f in range(20)]
        for e in range(5):
            for rp in range(4):
                store_half(base_ref, e * 4 + rp, h, solve(h, diag_ref, e, rp, flow))
        for q in range(2):
            weight = [None] * 20
            for g in range(5):
                weight[g * 4] = weight_ref[pl.ds(g * 32 + h * 16 + q, 8, stride=2), :]
            for e in range(5):
                row = (e * 2 + q) * 16 + h * 8
                map_ref[row : row + 8, :] = solve(h, diag_ref, e, 0, weight)
        coupling = couple(h, src_ref, (g0, g1, g2, g3), near_ref, jac_ref)
        add_spin(h, coupling, src_ref, freq)
        for e in range(5):
            for rp in range(4):
                f = e * 4 + rp
                store_half(pre_ref, f, h, load_half(base_ref, f, h) - solve(h, diag_ref, e, rp, coupling))


def wall_kernel(freq_ref, recv_ref, send_ref, pre_ref, base_ref, map_ref, it_ref, rhs_ref, h0, h1, h2, h3, a_ref, b_ref):
    freq = own_freq(freq_ref)
    sources = recv_ref.shape[0] // 9
    iota16 = lax.broadcasted_iota(jnp.int32, (16, LANES), 0)
    iota_l = lax.broadcasted_iota(jnp.int32, (LANES, LANES), 0)
    for s in range(sources):
        lanes = slice(s * LANES, (s + 1) * LANES)
        cell = bcast(recv_ref, s * 9 + 8).astype(jnp.int32)
        tile, lane = cell >> 7, cell & 127
        mask = jnp.where(iota16 == jnp.concatenate([tile] * 2, 0), 1.0, 0.0).astype(BF16)
        b_ref[:, lanes] = jnp.where(iota_l == jnp.concatenate([lane] * 16, 0), 1.0, 0.0).astype(BF16)
        for v in range(8):
            x = bcast(recv_ref, s * 9 + v)
            hi = x.astype(BF16)
            lo = (x - hi.astype(F32)).astype(BF16)
            a_ref[v * 16 : v * 16 + 16, lanes] = jnp.concatenate([hi, hi], 0) * mask
            a_ref[LANES + v * 16 : LANES + v * 16 + 16, lanes] = jnp.concatenate([lo, lo], 0) * mask
    both = lax.dot_general(a_ref[...], b_ref[...], NT, preferred_element_type=F32)
    wall = both[:LANES] + both[LANES:]
    for h in range(2):
        w = [wall[v * 16 + h * 8 : v * 16 + h * 8 + 8] for v in range(8)]
        velocity = [-freq[0] * w[2], -freq[1] * w[3], freq[0] * w[0], freq[1] * w[1]]
        for e in range(5):
            m0 = map_ref[e * 32 + h * 8 : e * 32 + h * 8 + 8, :]
            m1 = map_ref[e * 32 + 16 + h * 8 : e * 32 + 24 + h * 8, :]
            for rp in range(4):
                f = e * 4 + rp
                term = m0 * velocity[rp] + m1 * w[4 + rp]
                store_half(it_ref, f, h, load_half(pre_ref, f, h) + term)
                store_half(rhs_ref, f, h, load_half(base_ref, f, h) + term)
    pick_rows(it_ref, send_ref, (h0, h1, h2, h3))


def last_kernel(freq_ref, src_ref, g0, g1, g2, g3, near_ref, jac_ref, diag_ref, rhs_ref, out_ref):
    freq = own_freq(freq_ref)
    for h in range(2):
        coupling = couple(h, src_ref, (g0, g1, g2, g3), near_ref, jac_ref)
        add_spin(h, coupling, src_ref, freq)
        for e in range(5):
            for rp in range(4):
                f = e * 4 + rp
                store_half(out_ref, f, h, load_half(rhs_ref, f, h) - solve(h, diag_ref, e, rp, coupling))


def smem_call(body, operands, outs, scratch=()):
    specs = [pl.BlockSpec(memory_space=pltpu.SMEM)] + [pl.BlockSpec(memory_space=pltpu.VMEM)] * (
        len(operands) - 1
    )
    return pl.pallas_call(
        body,
        out_shape=[jax.ShapeDtypeStruct(shape, dtype) for shape, dtype in outs],
        in_specs=specs,
        scratch_shapes=list(scratch),
        compiler_params=pltpu.CompilerParams(vmem_limit_bytes=56 << 20),
    )(*operands)


def to_rows(field):
    lead = field.shape[:-2]
    inner = field.reshape(*lead, 2, field.shape[-1] // LANES, LANES)
    return jnp.swapaxes(inner, -3, -2).reshape(-1, LANES)


def from_rows(rows, shape):
    inner = rows.reshape(*shape[:-2], shape[-1] // LANES, 2, LANES)
    return jnp.swapaxes(inner, -3, -2).reshape(shape)


def exchange(blocks):
    return [
        from_behind(block, "dom", by) for block, by in zip(blocks, (1, -1, 2, -2), strict=True)
    ]


def shards(
    spline_blocks,
    modal_coeff,
    frequency,
    face_dest,
    face_cell,
    wall_weight,
    flow_rhs,
    previous,
    diag_inverse,
    off_jacobian,
    neighbor,
    send_list,
):
    dom = lax.axis_size("dom")
    halo = [((40, LANES), F32)] * 4
    coef = modal_coeff.reshape(64, 2, 4, 2).transpose(2, 1, 3, 0).reshape(16, 64)
    faces = kernel_call(face_kernel, [((4, 8, 1024), F32)])(coef, spline_blocks)[0]
    faces = lax.all_to_all(faces, "rep", split_axis=0, concat_axis=0, tiled=True)
    send = kernel_call(
        dispatch_kernel,
        [((dom * 9, LANES), F32)],
        [
            pltpu.VMEM((32 * dom, LANES), BF16),
            pltpu.VMEM((18 * dom, 4096), BF16),
            pltpu.VMEM((LANES, 4096), BF16),
        ],
    )(faces, face_dest.reshape(32, LANES), face_cell.reshape(32, LANES))[0]
    recv = lax.all_to_all(send, "dom", split_axis=0, concat_axis=0, tiled=True)

    prev = to_rows(previous)
    rows_out = send_list.reshape(8, LANES)
    picked = kernel_call(pick_kernel, halo)(prev, rows_out)
    ghosts = exchange(picked)
    near = neighbor.reshape(96, LANES)
    jac = off_jacobian.astype(F32).reshape(2400, LANES)
    diag = diag_inverse.reshape(400, LANES)
    field = ((320, LANES), F32)
    pre, base, wall_map = smem_call(
        first_kernel,
        (frequency, prev, *ghosts, near, jac, diag, to_rows(flow_rhs), to_rows(wall_weight)),
        [field, field, ((160, LANES), F32)],
    )
    it, rhs, *picked = smem_call(
        wall_kernel,
        (frequency, recv, rows_out, pre, base, wall_map),
        [field, field, *halo],
        [pltpu.VMEM((2 * LANES, dom * LANES), BF16), pltpu.VMEM((LANES, dom * LANES), BF16)],
    )
    ghosts = exchange(picked)
    out = smem_call(last_kernel, (frequency, it, *ghosts, near, jac, diag, rhs), [field])[0]
    return from_rows(out, flow_rhs.shape)


def solution(mesh):
    return jax.shard_map(
        shards,
        mesh=mesh,
        in_specs=(
            P(("dom", "rep"), None, None, None),
            P(),
            P(),
            P("dom", None),
            P("dom"),
            P(None, None, "dom"),
            P(None, None, "rep", "dom"),
            P(None, None, "rep", "dom"),
            P(None, None, "dom"),
            P(None, None, None, "dom"),
            P(None, "dom"),
            P(None, "dom"),
        ),
        out_specs=P(None, None, "rep", "dom"),
        check_vma=False,
    )
```

```python
import jax
import jax.numpy as jnp
from jax import lax
from jax.experimental import pallas as pl
from jax.experimental.pallas import tpu as pltpu
from jax.sharding import PartitionSpec as P

F32 = jnp.float32
BF16 = jnp.bfloat16
LANES = 128
NT = (((1,), (1,)), ((), ()))


def from_behind(value, axis, by):
    length = lax.axis_size(axis)
    return lax.ppermute(value, axis, [(i, (i + by) % length) for i in range(length)])


def kernel_call(body, outs, scratch=()):
    return pl.pallas_call(
        body,
        out_shape=[jax.ShapeDtypeStruct(shape, dtype) for shape, dtype in outs],
        scratch_shapes=list(scratch),
        compiler_params=pltpu.CompilerParams(vmem_limit_bytes=56 << 20),
    )


def bcast(ref, row, rows=8):
    return ref[pl.ds(row, rows, stride=0), :]


def face_kernel(coef_ref, spline_ref, out_ref):
    coef = coef_ref[...]
    blocks = spline_ref.shape[0]
    for k in range(blocks):
        for q in range(2):
            v = jnp.dot(coef, spline_ref[k, q], preferred_element_type=F32)
            for y in range(4):
                for r in range(2):
                    at = q * 4 + r * 2
                    out_ref[y, at : at + 2, k * LANES : (k + 1) * LANES] = v[
                        r * 8 + y * 2 : r * 8 + y * 2 + 2
                    ]


def split_rows(x):
    hi = x.astype(BF16).astype(F32)
    return hi, x - hi


def iota_rows(rows):
    return lax.broadcasted_iota(jnp.int32, (rows, LANES), 0).astype(F32).astype(BF16)


def one_hot(iota, row16):
    full = jnp.concatenate([row16] * (iota.shape[0] // 16), 0)
    return jnp.where(iota == full, jnp.ones_like(iota), jnp.zeros_like(iota))


def slot_kernel(dest_ref, slot_ref):
    doms = 64
    tiles = dest_ref.shape[0]
    iota_d = lax.broadcasted_iota(jnp.int32, (doms, LANES), 0)
    iota_p = lax.broadcasted_iota(jnp.int32, (LANES, LANES), 0)
    iota_l = lax.broadcasted_iota(jnp.int32, (LANES, LANES), 1)
    upper = jnp.concatenate(
        [jnp.where(iota_p <= iota_l, 1.0, 0.0), jnp.ones((LANES, LANES), F32)], axis=1
    ).astype(BF16)
    carry = jnp.zeros((doms, LANES), F32)
    for t in range(tiles):
        dest = bcast(dest_ref, t, 8)
        one = jnp.where(iota_d == jnp.concatenate([dest] * 8, 0), 1.0, 0.0)
        counts = jnp.dot(one.astype(BF16), upper, preferred_element_type=F32)
        place = counts[:, :LANES] + carry
        carry = carry + counts[:, LANES:]
        rank = jnp.sum(one * place, axis=0, keepdims=True).astype(jnp.int32) - 1
        slot_ref[t : t + 1, :] = (dest[:1] & 1) * LANES + rank


def store_split(hl_ref, at, x):
    hi8, lo8 = split_rows(x)
    hl_ref[at : at + 8, :] = hi8
    hl_ref[at + 8 : at + 16, :] = lo8


def narrow(x):
    return x.astype(F32).astype(BF16)


CHUNK = 8


def add_to(total, parts_a, parts_b):
    a = jnp.concatenate([jnp.concatenate(p, axis=0) for p in parts_a], axis=1)
    b = jnp.concatenate(parts_b, axis=1)
    product = lax.dot_general(a, b, NT, preferred_element_type=F32)
    return product if total is None else total + product


def dispatch_kernel(vals_ref, dest_ref, slot_ref, cell_ref, out_ref, hl_ref):
    pairs = out_ref.shape[0] // 18
    tiles = dest_ref.shape[0]
    iota_b = iota_rows(2 * LANES)
    iota_a = iota_rows(pairs)
    per_rep = tiles // 4
    for t in range(tiles):
        part = slice((t % per_rep) * LANES, (t % per_rep + 1) * LANES)
        store_split(hl_ref, t * 16, vals_ref[t // per_rep, :, part])
    total = None
    for c in range(0, tiles, CHUNK):
        parts_a, parts_b = [], []
        for t in range(c, c + CHUNK):
            parts_b.append(one_hot(iota_b, narrow(bcast(slot_ref, t, 16))))
            mask = one_hot(iota_a, narrow(bcast(dest_ref, t, 16) >> 1))
            cell = bcast(cell_ref, t, 16)
            rows = [bcast(hl_ref, t * 16 + v, 16).astype(BF16) for v in range(16)]
            rows = rows[:8] + [narrow((cell >> 7) << 7)] + rows[8:] + [narrow(cell & 127)]
            parts_a.append([jnp.concatenate([row] * (pairs // 16), 0) * mask for row in rows])
        total = add_to(total, parts_a, parts_b)
    for v in range(9):
        both = total[v * pairs : (v + 1) * pairs] + total[(9 + v) * pairs : (10 + v) * pairs]
        for d in range(2):
            out_ref[pl.ds(d * 9 + v, pairs, stride=18), :] = both[:, d * LANES : (d + 1) * LANES]


def field_row(f, t):
    return (f // 2) * 32 + t * 2 + f % 2


def load_half(ref, f, h):
    return ref[pl.ds(field_row(f, 8 * h), 8, stride=2), :]


def store_half(ref, f, h, value):
    ref[pl.ds(field_row(f, 8 * h), 8, stride=2), :] = value


def lane_take(row, lanes):
    return jnp.take_along_axis(row, lanes, axis=1, mode="promise_in_bounds")


def pick_rows(src_ref, send_ref, out_refs):
    idx = send_ref[...]
    hi, lo = idx >> 7, idx & 127
    masks = [hi == t for t in range(16)]
    for f in range(20):
        acc = lane_take(bcast(src_ref, field_row(f, 0)), lo)
        for t in range(1, 16):
            acc = jnp.where(masks[t], lane_take(bcast(src_ref, field_row(f, t)), lo), acc)
        for k in range(4):
            out_refs[k][f * 2 : f * 2 + 2, :] = acc[2 * k : 2 * k + 2]


def pick_kernel(src_ref, send_ref, *out_refs):
    pick_rows(src_ref, send_ref, out_refs)


def part_row(f):
    return (f // 2) * 16 + f % 2


def load_part(ref, f):
    return ref[pl.ds(part_row(f), 8, stride=2), :]


def store_part(ref, f, value):
    ref[pl.ds(part_row(f), 8, stride=2), :] = value


def couple(first_tile, rows_of, near_ref, jac_ref, beside_ref):
    coupling = [None] * 20
    tiles = len(rows_of(0))
    for step_at in range(7):
        if step_at < 6:
            idx = near_ref[step_at * 8 : step_at * 8 + 8, :]
            hi, lo = idx >> 7, idx & 127
            masks = [hi == first_tile + t for t in range(tiles)]
            for f in range(20):
                acc = jnp.zeros((8, LANES), F32)
                for t, (ref, row) in enumerate(rows_of(f)):
                    acc = jnp.where(masks[t], lane_take(bcast(ref, row), lo), acc)
                beside_ref[(step_at * 20 + f) * 8 : (step_at * 20 + f) * 8 + 8, :] = acc
        j = step_at - 1
        if j >= 0:
            for g in range(5):
                at = (j * 20 + g * 4) * 8
                beside = [beside_ref[at + rp * 8 : at + rp * 8 + 8, :] for rp in range(4)]
                for e in range(5):
                    row = ((j * 5 + e) * 5 + g) * 8
                    jac = jac_ref[row : row + 8, :]
                    for rp in range(4):
                        term = jac * beside[rp]
                        at_e = e * 4 + rp
                        coupling[at_e] = term if coupling[at_e] is None else coupling[at_e] + term
    return coupling


def local_coupling(h, freq, src_ref, near_ref, jac_ref, beside_ref):
    coupling = couple(0, lambda f: [(src_ref, field_row(f, t)) for t in range(16)], near_ref, jac_ref, beside_ref)
    for g in range(5):
        for p in range(2):
            re, im = g * 4 + p, g * 4 + 2 + p
            coupling[re] = coupling[re] - freq[p] * load_half(src_ref, im, h)
            coupling[im] = coupling[im] + freq[p] * load_half(src_ref, re, h)
    return coupling


def own_freq(freq_ref):
    first = lax.axis_index("rep") * 2
    return [freq_ref[first], freq_ref[first + 1]]


def solve(diag_ref, e, rp, parts):
    total = None
    for g in range(5):
        row = (e * 5 + g) * 8
        term = diag_ref[row : row + 8, :] * parts[g * 4 + rp]
        total = term if total is None else total + term
    return total


def untile(tables_ref, base, tiles_of, count, tile_count, write):
    for t in range(tile_count):
        tables_ref[base + t * 8 : base + t * 8 + count, :] = tiles_of(slice(t * LANES, (t + 1) * LANES))
    for i in range(count):
        write(i, tables_ref[pl.ds(base + i, tile_count, stride=8), :])


def first_local(h):
    def body(freq_ref, src_ref, near_in, jac_in, diag_in, flow_ref, weight_ref, near_ref, jac_ref, diag_ref, part_ref, base_ref, map_ref, tables_ref, beside_ref):
        freq = own_freq(freq_ref)

        def write_near(j, rows):
            near_ref[j * 8 : j * 8 + 8, :] = rows

        untile(tables_ref, 0, lambda lanes: near_in[:, lanes].astype(F32), 6, 8, lambda j, rows: write_near(j, rows.astype(jnp.int32)))
        for e in range(5):
            for g in range(5):

                def write_jac(j, rows, e=e, g=g):
                    at = ((j * 5 + e) * 5 + g) * 8
                    jac_ref[at : at + 8, :] = rows

                untile(tables_ref, (6 + e * 5 + g) * 64, lambda lanes, e=e, g=g: jac_in[e, g, :, lanes].astype(F32), 6, 8, write_jac)

            def write_diag(g, rows, e=e):
                at = (e * 5 + g) * 8
                diag_ref[at : at + 8, :] = rows

            untile(tables_ref, (1 + e) * 64, lambda lanes, e=e: diag_in[e, :, lanes], 5, 8, write_diag)
        flow = [load_half(flow_ref, f, h) for f in range(20)]
        for f in range(20):
            store_part(base_ref, f, solve(diag_ref, f // 4, f % 4, flow))
        for q in range(2):
            weight = [None] * 20
            for g in range(5):
                weight[g * 4] = weight_ref[pl.ds(g * 32 + h * 16 + q, 8, stride=2), :]
            for e in range(5):
                row = (e * 2 + q) * 8
                map_ref[row : row + 8, :] = solve(diag_ref, e, 0, weight)
        coupling = local_coupling(h, freq, src_ref, near_ref, jac_ref, beside_ref)
        for f in range(20):
            store_part(part_ref, f, load_part(base_ref, f) - solve(diag_ref, f // 4, f % 4, coupling))

    return body


def wall_terms(freq, wall_of, map_ref):
    w = [wall_of(v) for v in range(8)]
    velocity = [-freq[0] * w[2], -freq[1] * w[3], freq[0] * w[0], freq[1] * w[1]]
    terms = []
    for e in range(5):
        m0 = map_ref[e * 16 : e * 16 + 8, :]
        m1 = map_ref[e * 16 + 8 : e * 16 + 16, :]
        terms += [m0 * velocity[rp] + m1 * w[4 + rp] for rp in range(4)]
    return terms


def last_local(h):
    def body(freq_ref, src_ref, near_ref, jac_ref, diag_ref, base_ref, map_ref, wall_ref, part_ref, beside_ref):
        freq = own_freq(freq_ref)
        terms = wall_terms(freq, lambda v: wall_ref[v * 16 + h * 8 : v * 16 + h * 8 + 8, :], map_ref)
        for f in range(20):
            store_part(part_ref, f, load_part(base_ref, f) + terms[f])
        coupling = local_coupling(h, freq, src_ref, near_ref, jac_ref, beside_ref)
        for f in range(20):
            store_part(part_ref, f, load_part(part_ref, f) - solve(diag_ref, f // 4, f % 4, coupling))

    return body


def ghost_kernel(g0, g1, g2, g3, *refs):
    ghosts = (g0, g1, g2, g3)
    out_ref, beside_ref = refs[8:]
    for h in range(2):
        near_ref, jac_ref, diag_ref, part_ref = refs[h * 4 : h * 4 + 4]
        coupling = couple(
            16, lambda f: [(ghosts[t // 2], f * 2 + t % 2) for t in range(8)], near_ref, jac_ref, beside_ref.at[h]
        )
        for f in range(20):
            store_half(out_ref, f, h, load_part(part_ref, f) - solve(diag_ref, f // 4, f % 4, coupling))


def wall_kernel(freq_ref, recv_ref, send_ref, pre_ref, map0, map1, it_ref, wall_ref, h0, h1, h2, h3, hl_ref):
    freq = own_freq(freq_ref)
    sources = recv_ref.shape[0] // 9
    iota_a = iota_rows(16)
    iota_b = iota_rows(LANES)
    for s in range(sources):
        store_split(hl_ref, s * 16, recv_ref[s * 9 : s * 9 + 8, :])
    total = None
    for c in range(0, sources, CHUNK):
        parts_a, parts_b = [], []
        for s in range(c, c + CHUNK):
            cell = bcast(recv_ref, s * 9 + 8, 16).astype(jnp.int32)
            mask = one_hot(iota_a, narrow(cell >> 7))
            parts_b.append(one_hot(iota_b, narrow(cell & 127)))
            parts_a.append([bcast(hl_ref, s * 16 + v, 16).astype(BF16) * mask for v in range(16)])
        total = add_to(total, parts_a, parts_b)
    wall = total[:LANES] + total[LANES:]
    wall_ref[...] = wall
    for h in range(2):
        terms = wall_terms(freq, lambda v: wall[v * 16 + h * 8 : v * 16 + h * 8 + 8], (map0, map1)[h])
        for f in range(20):
            store_half(it_ref, f, h, load_half(pre_ref, f, h) + terms[f])
    pick_rows(it_ref, send_ref, (h0, h1, h2, h3))


def smem_call(body, operands, outs, scratch=(), specs=None):
    specs = specs or [pl.BlockSpec()] * (len(operands) - 1)
    return pl.pallas_call(
        body,
        grid=(1,),
        out_shape=[jax.ShapeDtypeStruct(shape, dtype) for shape, dtype in outs],
        in_specs=[pl.BlockSpec(memory_space=pltpu.SMEM), *specs],
        scratch_shapes=list(scratch),
        compiler_params=pltpu.CompilerParams(vmem_limit_bytes=56 << 20),
    )(*operands)


def to_rows(field):
    lead = field.shape[:-2]
    inner = field.reshape(*lead, 2, field.shape[-1] // LANES, LANES)
    return jnp.swapaxes(inner, -3, -2).reshape(-1, LANES)


def from_rows(rows, shape):
    inner = rows.reshape(*shape[:-2], shape[-1] // LANES, 2, LANES)
    return jnp.swapaxes(inner, -3, -2).reshape(shape)


ORDER = ((2, 2), (0, 1), (3, -2), (1, -1))


def exchange(blocks):
    ghosts = [None] * 4
    for k, by in ORDER:
        ghosts[k] = from_behind(blocks[k], "dom", by)
    return ghosts


def step(
    spline_blocks,
    modal_coeff,
    frequency,
    face_dest,
    face_cell,
    wall_weight,
    flow_rhs,
    previous,
    diag_inverse,
    off_jacobian,
    neighbor,
    send_list,
):
    dom = lax.axis_size("dom")
    halo = [((40, LANES), F32)] * 4
    part, small, field = ((160, LANES), F32), ((80, LANES), F32), ((320, LANES), F32)
    dest = face_dest.reshape(32, LANES)
    faces = kernel_call(face_kernel, [((4, 8, 1024), F32)])(modal_coeff.transpose(1, 2, 0).reshape(16, 64), spline_blocks)[0]
    faces = lax.all_to_all(faces, "rep", split_axis=0, concat_axis=0, tiled=True)
    slot = kernel_call(slot_kernel, [((32, LANES), jnp.int32)])(dest)[0]
    prev = to_rows(previous)
    rows_out = send_list.reshape(8, LANES)
    picked = kernel_call(pick_kernel, halo)(prev, rows_out)
    ghosts = exchange(picked)
    send = kernel_call(
        dispatch_kernel,
        [((dom * 9, LANES), F32)],
        [pltpu.VMEM((512, LANES), F32)],
    )(faces, dest, slot, face_cell.reshape(32, LANES))[0]
    recv = lax.all_to_all(send.reshape(dom, 9, 1, LANES), "dom", split_axis=0, concat_axis=0, tiled=True)
    recv = recv.reshape(dom * 9, LANES)

    half = neighbor.shape[1] // 2
    jac_in = off_jacobian.transpose(1, 2, 0, 3)
    flow, weight = to_rows(flow_rhs), to_rows(wall_weight)
    beside = pltpu.VMEM((960, LANES), F32)
    tables, parts, bases, maps = [], [], [], []
    for h in range(2):
        specs = [
            pl.BlockSpec(),
            pl.BlockSpec((6, half), lambda i, h=h: (0, h)),
            pl.BlockSpec((5, 5, 6, half), lambda i, h=h: (0, 0, 0, h)),
            pl.BlockSpec((5, 5, half), lambda i, h=h: (0, 0, h)),
            pl.BlockSpec(),
            pl.BlockSpec(),
        ]
        near, jac, diag, p, b, m = smem_call(
            first_local(h),
            (frequency, prev, neighbor, jac_in, diag_inverse, flow, weight),
            [((48, LANES), jnp.int32), ((1200, LANES), F32), ((200, LANES), F32), part, part, small],
            [pltpu.VMEM((31 * 64, LANES), F32), beside],
            specs,
        )
        tables.append((near, jac, diag))
        parts.append(p)
        bases.append(b)
        maps.append(m)
    both_beside = [pltpu.VMEM((2, 960, LANES), F32)]
    pre = kernel_call(ghost_kernel, [field], both_beside)(*ghosts, *tables[0], parts[0], *tables[1], parts[1])[0]
    it, wall, *picked = smem_call(
        wall_kernel,
        (frequency, recv, rows_out, pre, maps[0], maps[1]),
        [field, ((LANES, LANES), F32), *halo],
        [pltpu.VMEM((dom * 16, LANES), F32)],
    )
    ghosts = exchange(picked)
    parts = []
    for h in range(2):
        parts.append(
            smem_call(last_local(h), (frequency, it, *tables[h], bases[h], maps[h], wall), [part], [beside])[0]
        )
    out = kernel_call(ghost_kernel, [field], both_beside)(*ghosts, *tables[0], parts[0], *tables[1], parts[1])[0]
    return from_rows(out, flow_rhs.shape)


def solution(mesh):
    return jax.shard_map(
        step,
        mesh=mesh,
        in_specs=(
            P(("dom", "rep"), None, None, None),
            P(),
            P(),
            P("dom", None),
            P("dom"),
            P(None, None, "dom"),
            P(None, None, "rep", "dom"),
            P(None, None, "rep", "dom"),
            P(None, None, "dom"),
            P(None, None, None, "dom"),
            P(None, "dom"),
            P(None, "dom"),
        ),
        out_specs=P(None, None, "rep", "dom"),
        check_vma=False,
    )
```

```python
import jax
import jax.numpy as jnp
from jax import lax
from jax.experimental import pallas as pl
from jax.experimental.pallas import tpu as pltpu
from jax.sharding import PartitionSpec as P

F32 = jnp.float32
BF16 = jnp.bfloat16
LANES = 128
NT = (((1,), (1,)), ((), ()))


def from_behind(value, axis, by):
    length = lax.axis_size(axis)
    return lax.ppermute(value, axis, [(i, (i + by) % length) for i in range(length)])


def call(body, operands, outs, scratch=(), specs=None, smem=0, near_out=()):
    arrays, in_specs = [], []
    for place, operand in enumerate(operands):
        if place < smem:
            in_specs.append(pl.BlockSpec(memory_space=pltpu.SMEM))
            arrays.append(operand)
        elif isinstance(operand, tuple):
            in_specs.append(pl.BlockSpec(memory_space=pltpu.VMEM))
            arrays.append(pltpu.with_memory_space_constraint(operand[0], pltpu.VMEM))
        else:
            in_specs.append((specs or {}).get(place, pl.BlockSpec()))
            arrays.append(operand)
    shapes, out_specs = [], []
    for place, (shape, dtype) in enumerate(outs):
        if place in near_out:
            shapes.append(pltpu.VMEM(shape, dtype))
            out_specs.append(pl.BlockSpec(memory_space=pltpu.VMEM))
        else:
            shapes.append(jax.ShapeDtypeStruct(shape, dtype))
            out_specs.append(pl.BlockSpec())
    return pl.pallas_call(
        body,
        grid=(1,),
        out_shape=shapes,
        in_specs=in_specs,
        out_specs=out_specs,
        scratch_shapes=list(scratch),
        compiler_params=pltpu.CompilerParams(vmem_limit_bytes=24 << 20),
    )(*arrays)


def bcast(ref, row, rows=8):
    return ref[pl.ds(row, rows, stride=0), :]


def face_kernel(coef_ref, spline_ref, out_ref):
    coef = coef_ref[...]
    blocks = spline_ref.shape[0]
    for k in range(blocks):
        for q in range(2):
            v = jnp.dot(coef, spline_ref[k, q], preferred_element_type=F32)
            for y in range(4):
                for r in range(2):
                    at = q * 4 + r * 2
                    out_ref[y, at : at + 2, k * LANES : (k + 1) * LANES] = v[
                        r * 8 + y * 2 : r * 8 + y * 2 + 2
                    ]


def split_rows(x):
    hi = x.astype(BF16).astype(F32)
    return hi, x - hi


def iota_rows(rows):
    return lax.broadcasted_iota(jnp.int32, (rows, LANES), 0).astype(F32).astype(BF16)


def one_hot(iota, row16):
    full = jnp.concatenate([row16] * (iota.shape[0] // 16), 0)
    return jnp.where(iota == full, jnp.ones_like(iota), jnp.zeros_like(iota))


def slot_kernel(dest_ref, slot_ref):
    doms = 64
    tiles = dest_ref.shape[0]
    iota_d = lax.broadcasted_iota(jnp.int32, (doms, LANES), 0)
    iota_p = lax.broadcasted_iota(jnp.int32, (LANES, LANES), 0)
    iota_l = lax.broadcasted_iota(jnp.int32, (LANES, LANES), 1)
    upper = jnp.concatenate(
        [jnp.where(iota_p <= iota_l, 1.0, 0.0), jnp.ones((LANES, LANES), F32)], axis=1
    ).astype(BF16)
    carry = jnp.zeros((doms, LANES), F32)
    for t in range(tiles):
        dest = bcast(dest_ref, t, 8)
        one = jnp.where(iota_d == jnp.concatenate([dest] * 8, 0), 1.0, 0.0)
        counts = jnp.dot(one.astype(BF16), upper, preferred_element_type=F32)
        place = counts[:, :LANES] + carry
        carry = carry + counts[:, LANES:]
        rank = jnp.sum(one * place, axis=0, keepdims=True).astype(jnp.int32) - 1
        slot_ref[t : t + 1, :] = (dest[:1] & 1) * LANES + rank


def store_split(hl_ref, at, x):
    hi8, lo8 = split_rows(x)
    hl_ref[at : at + 8, :] = hi8
    hl_ref[at + 8 : at + 16, :] = lo8


def narrow(x):
    return x.astype(F32).astype(BF16)


CHUNK = 8


def add_to(total, parts_a, parts_b):
    a = jnp.concatenate([jnp.concatenate(p, axis=0) for p in parts_a], axis=1)
    b = jnp.concatenate(parts_b, axis=1)
    product = lax.dot_general(a, b, NT, preferred_element_type=F32)
    return product if total is None else total + product


def dispatch_kernel(vals_ref, dest_ref, slot_ref, cell_ref, out_ref, hl_ref):
    pairs = out_ref.shape[0] // 18
    tiles = dest_ref.shape[0]
    iota_b = iota_rows(2 * LANES)
    iota_a = iota_rows(pairs)
    per_rep = tiles // 4
    for t in range(tiles):
        part = slice((t % per_rep) * LANES, (t % per_rep + 1) * LANES)
        store_split(hl_ref, t * 16, vals_ref[t // per_rep, :, part])
    total = None
    for c in range(0, tiles, CHUNK):
        parts_a, parts_b = [], []
        for t in range(c, c + CHUNK):
            parts_b.append(one_hot(iota_b, narrow(bcast(slot_ref, t, 16))))
            mask = one_hot(iota_a, narrow(bcast(dest_ref, t, 16) >> 1))
            cell = bcast(cell_ref, t, 16)
            rows = [bcast(hl_ref, t * 16 + v, 16).astype(BF16) for v in range(16)]
            rows = rows[:8] + [narrow((cell >> 7) << 7)] + rows[8:] + [narrow(cell & 127)]
            parts_a.append([jnp.concatenate([row] * (pairs // 16), 0) * mask for row in rows])
        total = add_to(total, parts_a, parts_b)
    for v in range(9):
        both = total[v * pairs : (v + 1) * pairs] + total[(9 + v) * pairs : (10 + v) * pairs]
        for d in range(2):
            out_ref[pl.ds(d * 9 + v, pairs, stride=18), :] = both[:, d * LANES : (d + 1) * LANES]


def field_row(f, t):
    return (f // 2) * 32 + t * 2 + f % 2


def load_half(ref, f, h):
    return ref[pl.ds(field_row(f, 8 * h), 8, stride=2), :]


def store_half(ref, f, h, value):
    ref[pl.ds(field_row(f, 8 * h), 8, stride=2), :] = value


def lane_take(row, lanes):
    return jnp.take_along_axis(row, lanes, axis=1, mode="promise_in_bounds")


def pick_rows(src_ref, send_ref, out_refs):
    idx = send_ref[...]
    hi, lo = idx >> 7, idx & 127
    masks = [hi == t for t in range(16)]
    for f in range(20):
        acc = lane_take(bcast(src_ref, field_row(f, 0)), lo)
        for t in range(1, 16):
            acc = jnp.where(masks[t], lane_take(bcast(src_ref, field_row(f, t)), lo), acc)
        for k in range(4):
            out_refs[k][f * 2 : f * 2 + 2, :] = acc[2 * k : 2 * k + 2]


def pick_kernel(src_ref, send_ref, *out_refs):
    pick_rows(src_ref, send_ref, out_refs)


def part_row(f):
    return (f // 2) * 16 + f % 2


def load_part(ref, f):
    return ref[pl.ds(part_row(f), 8, stride=2), :]


def store_part(ref, f, value):
    ref[pl.ds(part_row(f), 8, stride=2), :] = value


def couple(first_tile, rows_of, near_ref, jac_ref, beside_ref):
    coupling = [None] * 20
    tiles = len(rows_of(0))
    for step_at in range(7):
        if step_at < 6:
            idx = near_ref[step_at * 8 : step_at * 8 + 8, :]
            hi, lo = idx >> 7, idx & 127
            masks = [hi == first_tile + t for t in range(tiles)]
            for f in range(20):
                acc = jnp.zeros((8, LANES), F32)
                for t, (ref, row) in enumerate(rows_of(f)):
                    acc = jnp.where(masks[t], lane_take(bcast(ref, row), lo), acc)
                beside_ref[(step_at * 20 + f) * 8 : (step_at * 20 + f) * 8 + 8, :] = acc
        j = step_at - 1
        if j >= 0:
            for g in range(5):
                at = (j * 20 + g * 4) * 8
                beside = [beside_ref[at + rp * 8 : at + rp * 8 + 8, :] for rp in range(4)]
                for e in range(5):
                    row = ((j * 5 + e) * 5 + g) * 8
                    jac = jac_ref[row : row + 8, :]
                    for rp in range(4):
                        term = jac * beside[rp]
                        at_e = e * 4 + rp
                        coupling[at_e] = term if coupling[at_e] is None else coupling[at_e] + term
    return coupling


def local_coupling(h, freq, src_ref, near_ref, jac_ref, beside_ref):
    coupling = couple(0, lambda f: [(src_ref, field_row(f, t)) for t in range(16)], near_ref, jac_ref, beside_ref)
    for g in range(5):
        for p in range(2):
            re, im = g * 4 + p, g * 4 + 2 + p
            coupling[re] = coupling[re] - freq[p] * load_half(src_ref, im, h)
            coupling[im] = coupling[im] + freq[p] * load_half(src_ref, re, h)
    return coupling


def own_freq(freq_ref):
    first = lax.axis_index("rep") * 2
    return [freq_ref[first], freq_ref[first + 1]]


def solve(diag_ref, e, rp, parts):
    total = None
    for g in range(5):
        row = (e * 5 + g) * 8
        term = diag_ref[row : row + 8, :] * parts[g * 4 + rp]
        total = term if total is None else total + term
    return total


def untile(tables_ref, base, tiles_of, count, tile_count, write):
    for t in range(tile_count):
        tables_ref[base + t * 8 : base + t * 8 + count, :] = tiles_of(slice(t * LANES, (t + 1) * LANES))
    for i in range(count):
        write(i, tables_ref[pl.ds(base + i, tile_count, stride=8), :])


def first_local(h):
    def body(freq_ref, src_ref, near_in, jac_in, diag_in, flow_ref, weight_ref, near_ref, jac_ref, diag_ref, part_ref, base_ref, map_ref, tables_ref, beside_ref):
        freq = own_freq(freq_ref)

        def write_near(j, rows):
            near_ref[j * 8 : j * 8 + 8, :] = rows

        untile(tables_ref, 0, lambda lanes: near_in[:, lanes].astype(F32), 6, 8, lambda j, rows: write_near(j, rows.astype(jnp.int32)))
        for e in range(5):
            for g in range(5):

                def write_jac(j, rows, e=e, g=g):
                    at = ((j * 5 + e) * 5 + g) * 8
                    jac_ref[at : at + 8, :] = rows

                untile(tables_ref, (6 + e * 5 + g) * 64, lambda lanes, e=e, g=g: jac_in[e, g, :, lanes].astype(F32), 6, 8, write_jac)

            def write_diag(g, rows, e=e):
                at = (e * 5 + g) * 8
                diag_ref[at : at + 8, :] = rows

            untile(tables_ref, (1 + e) * 64, lambda lanes, e=e: diag_in[e, :, lanes], 5, 8, write_diag)
        flow = [load_half(flow_ref, f, h) for f in range(20)]
        for f in range(20):
            store_part(base_ref, f, solve(diag_ref, f // 4, f % 4, flow))
        for q in range(2):
            weight = [None] * 20
            for g in range(5):
                weight[g * 4] = weight_ref[pl.ds(g * 32 + h * 16 + q, 8, stride=2), :]
            for e in range(5):
                row = (e * 2 + q) * 8
                map_ref[row : row + 8, :] = solve(diag_ref, e, 0, weight)
        coupling = local_coupling(h, freq, src_ref, near_ref, jac_ref, beside_ref)
        for f in range(20):
            store_part(part_ref, f, load_part(base_ref, f) - solve(diag_ref, f // 4, f % 4, coupling))

    return body


def wall_terms(freq, wall_of, map_ref):
    w = [wall_of(v) for v in range(8)]
    velocity = [-freq[0] * w[2], -freq[1] * w[3], freq[0] * w[0], freq[1] * w[1]]
    terms = []
    for e in range(5):
        m0 = map_ref[e * 16 : e * 16 + 8, :]
        m1 = map_ref[e * 16 + 8 : e * 16 + 16, :]
        terms += [m0 * velocity[rp] + m1 * w[4 + rp] for rp in range(4)]
    return terms


def last_local(h):
    def body(freq_ref, src_ref, near_ref, jac_ref, diag_ref, base_ref, map_ref, wall_ref, part_ref, beside_ref):
        freq = own_freq(freq_ref)
        terms = wall_terms(freq, lambda v: wall_ref[v * 16 + h * 8 : v * 16 + h * 8 + 8, :], map_ref)
        for f in range(20):
            store_part(part_ref, f, load_part(base_ref, f) + terms[f])
        coupling = local_coupling(h, freq, src_ref, near_ref, jac_ref, beside_ref)
        for f in range(20):
            store_part(part_ref, f, load_part(part_ref, f) - solve(diag_ref, f // 4, f % 4, coupling))

    return body


def ghost_kernel(g0, g1, g2, g3, *refs):
    ghosts = (g0, g1, g2, g3)
    out_ref, beside_ref = refs[8:]
    for h in range(2):
        near_ref, jac_ref, diag_ref, part_ref = refs[h * 4 : h * 4 + 4]
        coupling = couple(
            16, lambda f: [(ghosts[t // 2], f * 2 + t % 2) for t in range(8)], near_ref, jac_ref, beside_ref.at[h]
        )
        for f in range(20):
            store_half(out_ref, f, h, load_part(part_ref, f) - solve(diag_ref, f // 4, f % 4, coupling))


def wall_kernel(freq_ref, recv_ref, send_ref, pre_ref, map0, map1, it_ref, wall_ref, h0, h1, h2, h3, hl_ref):
    freq = own_freq(freq_ref)
    sources = recv_ref.shape[0] // 9
    iota_a = iota_rows(16)
    iota_b = iota_rows(LANES)
    for s in range(sources):
        store_split(hl_ref, s * 16, recv_ref[s * 9 : s * 9 + 8, :])
    total = None
    for c in range(0, sources, CHUNK):
        parts_a, parts_b = [], []
        for s in range(c, c + CHUNK):
            cell = bcast(recv_ref, s * 9 + 8, 16).astype(jnp.int32)
            mask = one_hot(iota_a, narrow(cell >> 7))
            parts_b.append(one_hot(iota_b, narrow(cell & 127)))
            parts_a.append([bcast(hl_ref, s * 16 + v, 16).astype(BF16) * mask for v in range(16)])
        total = add_to(total, parts_a, parts_b)
    wall = total[:LANES] + total[LANES:]
    wall_ref[...] = wall
    for h in range(2):
        terms = wall_terms(freq, lambda v: wall[v * 16 + h * 8 : v * 16 + h * 8 + 8], (map0, map1)[h])
        for f in range(20):
            store_half(it_ref, f, h, load_half(pre_ref, f, h) + terms[f])
    pick_rows(it_ref, send_ref, (h0, h1, h2, h3))


def to_rows(field):
    lead = field.shape[:-2]
    inner = field.reshape(*lead, 2, field.shape[-1] // LANES, LANES)
    return jnp.swapaxes(inner, -3, -2).reshape(-1, LANES)


def from_rows(rows, shape):
    inner = rows.reshape(*shape[:-2], shape[-1] // LANES, 2, LANES)
    return jnp.swapaxes(inner, -3, -2).reshape(shape)


NEAR_FACE = (0,)
NEAR_PICK = range(4)
NEAR_SEND = (0,)
ORDER = ((2, 2), (0, 1), (3, -2), (1, -1))


def exchange(blocks):
    ghosts = [None] * 4
    for k, by in ORDER:
        ghosts[k] = from_behind(blocks[k], "dom", by)
    return ghosts


def step(
    spline_blocks,
    modal_coeff,
    frequency,
    face_dest,
    face_cell,
    wall_weight,
    flow_rhs,
    previous,
    diag_inverse,
    off_jacobian,
    neighbor,
    send_list,
):
    dom = lax.axis_size("dom")
    halo = [((40, LANES), F32)] * 4
    part, small, field = ((160, LANES), F32), ((80, LANES), F32), ((320, LANES), F32)
    dest = face_dest.reshape(32, LANES)
    coef = modal_coeff.transpose(1, 2, 0).reshape(16, 64)
    faces = call(face_kernel, (coef, spline_blocks), [((4, 8, 1024), F32)], near_out=NEAR_FACE)[0]
    faces = lax.all_to_all(faces, "rep", split_axis=0, concat_axis=0, tiled=True)
    slot = call(slot_kernel, (dest,), [((32, LANES), jnp.int32)], near_out=(0,))[0]
    prev = to_rows(previous)
    rows_out = send_list.reshape(8, LANES)
    picked = call(pick_kernel, (prev, rows_out), halo, near_out=NEAR_PICK)
    ghosts = exchange(picked)
    send = call(
        dispatch_kernel,
        ((faces,), dest, (slot,), face_cell.reshape(32, LANES)),
        [((dom * 9, LANES), F32)],
        [pltpu.VMEM((512, LANES), F32)],
        near_out=NEAR_SEND,
    )[0]
    recv = lax.all_to_all(send.reshape(dom, 9, 1, LANES), "dom", split_axis=0, concat_axis=0, tiled=True)
    recv = recv.reshape(dom * 9, LANES)

    half = neighbor.shape[1] // 2
    jac_in = off_jacobian.transpose(1, 2, 0, 3)
    flow, weight = to_rows(flow_rhs), to_rows(wall_weight)
    beside = pltpu.VMEM((960, LANES), F32)
    tables, parts, bases, maps = [], [], [], []
    for h in range(2):
        specs = {
            2: pl.BlockSpec((6, half), lambda i, h=h: (0, h)),
            3: pl.BlockSpec((5, 5, 6, half), lambda i, h=h: (0, 0, 0, h)),
            4: pl.BlockSpec((5, 5, half), lambda i, h=h: (0, 0, h)),
        }
        near, jac, diag, p, b, m = call(
            first_local(h),
            (frequency, prev, neighbor, jac_in, diag_inverse, flow, weight),
            [((48, LANES), jnp.int32), ((1200, LANES), F32), ((200, LANES), F32), part, part, small],
            [pltpu.VMEM((31 * 64, LANES), F32), beside],
            specs,
            smem=1,
            near_out=range(6),
        )
        tables += [(near,), (jac,), (diag,)]
        parts.append((p,))
        bases.append((b,))
        maps.append((m,))
    both_beside = [pltpu.VMEM((2, 960, LANES), F32)]

    def ghost_part(ghosts, parts, near_out):
        operands = (*[(g,) for g in ghosts], *tables[:3], parts[0], *tables[3:], parts[1])
        return call(ghost_kernel, operands, [field], both_beside, near_out=near_out)[0]

    pre = ghost_part(ghosts, parts, (0,))
    it, wall, *picked = call(
        wall_kernel,
        (frequency, (recv,), (rows_out,), (pre,), *maps),
        [field, ((LANES, LANES), F32), *halo],
        [pltpu.VMEM((dom * 16, LANES), F32)],
        smem=1,
        near_out=range(6),
    )
    ghosts = exchange(picked)
    parts = []
    for h in range(2):
        parts.append(
            call(
                last_local(h),
                (frequency, (it,), *tables[3 * h : 3 * h + 3], bases[h], maps[h], (wall,)),
                [part],
                [beside],
                smem=1,
                near_out=(0,),
            )
        )
    out = ghost_part(ghosts, [tuple(p) for p in parts], ())
    return from_rows(out, flow_rhs.shape)


def solution(mesh):
    return jax.shard_map(
        step,
        mesh=mesh,
        in_specs=(
            P(("dom", "rep"), None, None, None),
            P(),
            P(),
            P("dom", None),
            P("dom"),
            P(None, None, "dom"),
            P(None, None, "rep", "dom"),
            P(None, None, "rep", "dom"),
            P(None, None, "dom"),
            P(None, None, None, "dom"),
            P(None, "dom"),
            P(None, "dom"),
        ),
        out_specs=P(None, None, "rep", "dom"),
        check_vma=False,
    )
```

```python
import jax
import jax.numpy as jnp
from jax import lax
from jax.experimental import pallas as pl
from jax.experimental.pallas import tpu as pltpu
from jax.sharding import PartitionSpec as P

F32 = jnp.float32
BF16 = jnp.bfloat16
LANES = 128
NT = (((1,), (1,)), ((), ()))


def from_behind(value, axis, by):
    length = lax.axis_size(axis)
    return lax.ppermute(value, axis, [(i, (i + by) % length) for i in range(length)])


def call(body, operands, outs, scratch=(), specs=None, smem=0, near_out=()):
    arrays, in_specs = [], []
    for place, operand in enumerate(operands):
        if place < smem:
            in_specs.append(pl.BlockSpec(memory_space=pltpu.SMEM))
            arrays.append(operand)
        elif isinstance(operand, tuple):
            in_specs.append(pl.BlockSpec(memory_space=pltpu.VMEM))
            arrays.append(pltpu.with_memory_space_constraint(operand[0], pltpu.VMEM))
        else:
            in_specs.append((specs or {}).get(place, pl.BlockSpec()))
            arrays.append(operand)
    shapes, out_specs = [], []
    for place, (shape, dtype) in enumerate(outs):
        if place in near_out:
            shapes.append(pltpu.VMEM(shape, dtype))
            out_specs.append(pl.BlockSpec(memory_space=pltpu.VMEM))
        else:
            shapes.append(jax.ShapeDtypeStruct(shape, dtype))
            out_specs.append(pl.BlockSpec())
    return pl.pallas_call(
        body,
        grid=(1,),
        out_shape=shapes,
        in_specs=in_specs,
        out_specs=out_specs,
        scratch_shapes=list(scratch),
        compiler_params=pltpu.CompilerParams(vmem_limit_bytes=24 << 20),
    )(*arrays)


def bcast(ref, row, rows=8):
    return ref[pl.ds(row, rows, stride=0), :]


def face_kernel(coef_ref, spline_ref, out_ref):
    coef = coef_ref[...]
    blocks = spline_ref.shape[0]
    for k in range(blocks):
        for q in range(2):
            v = jnp.dot(coef, spline_ref[k, q], preferred_element_type=F32)
            for y in range(4):
                for r in range(2):
                    at = q * 4 + r * 2
                    out_ref[y, at : at + 2, k * LANES : (k + 1) * LANES] = v[
                        r * 8 + y * 2 : r * 8 + y * 2 + 2
                    ]


def split_rows(x):
    hi = x.astype(BF16).astype(F32)
    return hi, x - hi


def iota_rows(rows):
    return lax.broadcasted_iota(jnp.int32, (rows, LANES), 0).astype(F32).astype(BF16)


def one_hot(iota, row16):
    full = jnp.concatenate([row16] * (iota.shape[0] // 16), 0)
    return jnp.where(iota == full, jnp.ones_like(iota), jnp.zeros_like(iota))


def slot_kernel(freq_ref, dest_ref, slot_ref, plane_ref):
    doms = 64
    tiles = dest_ref.shape[0]
    first = lax.axis_index("rep") * 2
    for p in range(2):
        plane_ref[p * 8 : p * 8 + 8, :] = jnp.full((8, LANES), freq_ref[first + p], F32)
    iota_d = lax.broadcasted_iota(jnp.int32, (doms, LANES), 0)
    iota_p = lax.broadcasted_iota(jnp.int32, (LANES, LANES), 0)
    iota_l = lax.broadcasted_iota(jnp.int32, (LANES, LANES), 1)
    upper = jnp.concatenate(
        [jnp.where(iota_p <= iota_l, 1.0, 0.0), jnp.ones((LANES, LANES), F32)], axis=1
    ).astype(BF16)
    carry = jnp.zeros((doms, LANES), F32)
    for t in range(tiles):
        dest = bcast(dest_ref, t, 8)
        one = jnp.where(iota_d == jnp.concatenate([dest] * 8, 0), 1.0, 0.0)
        counts = jnp.dot(one.astype(BF16), upper, preferred_element_type=F32)
        place = counts[:, :LANES] + carry
        carry = carry + counts[:, LANES:]
        rank = jnp.sum(one * place, axis=0, keepdims=True).astype(jnp.int32) - 1
        slot_ref[t : t + 1, :] = (dest[:1] & 1) * LANES + rank


def store_split(hl_ref, at, x):
    hi8, lo8 = split_rows(x)
    hl_ref[at : at + 8, :] = hi8
    hl_ref[at + 8 : at + 16, :] = lo8


def narrow(x):
    return x.astype(F32).astype(BF16)


CHUNK = 8


def add_to(total, parts_a, parts_b):
    a = jnp.concatenate([jnp.concatenate(p, axis=0) for p in parts_a], axis=1)
    b = jnp.concatenate(parts_b, axis=1)
    product = lax.dot_general(a, b, NT, preferred_element_type=F32)
    return product if total is None else total + product


def dispatch_kernel(vals_ref, dest_ref, slot_ref, cell_ref, out_ref, hl_ref):
    pairs = out_ref.shape[0] // 18
    tiles = dest_ref.shape[0]
    iota_b = iota_rows(2 * LANES)
    iota_a = iota_rows(pairs)
    per_rep = tiles // 4
    for t in range(tiles):
        part = slice((t % per_rep) * LANES, (t % per_rep + 1) * LANES)
        store_split(hl_ref, t * 16, vals_ref[t // per_rep, :, part])
    total = None
    for c in range(0, tiles, CHUNK):
        parts_a, parts_b = [], []
        for t in range(c, c + CHUNK):
            parts_b.append(one_hot(iota_b, narrow(bcast(slot_ref, t, 16))))
            mask = one_hot(iota_a, narrow(bcast(dest_ref, t, 16) >> 1))
            cell = bcast(cell_ref, t, 16)
            rows = [bcast(hl_ref, t * 16 + v, 16).astype(BF16) for v in range(16)]
            rows = rows[:8] + [narrow((cell >> 7) << 7)] + rows[8:] + [narrow(cell & 127)]
            parts_a.append([jnp.concatenate([row] * (pairs // 16), 0) * mask for row in rows])
        total = add_to(total, parts_a, parts_b)
    for v in range(9):
        both = total[v * pairs : (v + 1) * pairs] + total[(9 + v) * pairs : (10 + v) * pairs]
        for d in range(2):
            out_ref[pl.ds(d * 9 + v, pairs, stride=18), :] = both[:, d * LANES : (d + 1) * LANES]


def field_row(f, t):
    return (f // 2) * 32 + t * 2 + f % 2


def load_half(ref, f, h):
    return ref[pl.ds(field_row(f, 8 * h), 8, stride=2), :]


def store_half(ref, f, h, value):
    ref[pl.ds(field_row(f, 8 * h), 8, stride=2), :] = value


def lane_take(row, lanes):
    return jnp.take_along_axis(row, lanes, axis=1, mode="promise_in_bounds")


def pick_rows(src_ref, send_ref, out_refs):
    idx = send_ref[...]
    hi, lo = idx >> 7, idx & 127
    masks = [hi == t for t in range(16)]
    for f in range(20):
        acc = lane_take(bcast(src_ref, field_row(f, 0)), lo)
        for t in range(1, 16):
            acc = jnp.where(masks[t], lane_take(bcast(src_ref, field_row(f, t)), lo), acc)
        for k in range(4):
            out_refs[k][f * 2 : f * 2 + 2, :] = acc[2 * k : 2 * k + 2]


def pick_kernel(src_ref, send_ref, *out_refs):
    pick_rows(src_ref, send_ref, out_refs)


def part_row(f):
    return (f // 2) * 16 + f % 2


def load_part(ref, f):
    return ref[pl.ds(part_row(f), 8, stride=2), :]


def store_part(ref, f, value):
    ref[pl.ds(part_row(f), 8, stride=2), :] = value


def couple(first_tile, rows_of, near_ref, jac_ref, beside_ref):
    coupling = [None] * 20
    tiles = len(rows_of(0))
    for step_at in range(7):
        if step_at < 6:
            idx = near_ref[step_at * 8 : step_at * 8 + 8, :]
            hi, lo = idx >> 7, idx & 127
            masks = [hi == first_tile + t for t in range(tiles)]
            for f in range(20):
                acc = jnp.zeros((8, LANES), F32)
                for t, (ref, row) in enumerate(rows_of(f)):
                    acc = jnp.where(masks[t], lane_take(bcast(ref, row), lo), acc)
                beside_ref[(step_at * 20 + f) * 8 : (step_at * 20 + f) * 8 + 8, :] = acc
        j = step_at - 1
        if j >= 0:
            for g in range(5):
                at = (j * 20 + g * 4) * 8
                beside = [beside_ref[at + rp * 8 : at + rp * 8 + 8, :] for rp in range(4)]
                for e in range(5):
                    row = ((j * 5 + e) * 5 + g) * 8
                    jac = jac_ref[row : row + 8, :]
                    for rp in range(4):
                        term = jac * beside[rp]
                        at_e = e * 4 + rp
                        coupling[at_e] = term if coupling[at_e] is None else coupling[at_e] + term
    return coupling


def local_coupling(h, freq, src_ref, near_ref, jac_ref, beside_ref):
    coupling = couple(0, lambda f: [(src_ref, field_row(f, t)) for t in range(16)], near_ref, jac_ref, beside_ref)
    for g in range(5):
        for p in range(2):
            re, im = g * 4 + p, g * 4 + 2 + p
            coupling[re] = coupling[re] - freq[p] * load_half(src_ref, im, h)
            coupling[im] = coupling[im] + freq[p] * load_half(src_ref, re, h)
    return coupling


def own_freq(plane_ref):
    return [plane_ref[0:8, :], plane_ref[8:16, :]]


def solve(diag_ref, e, rp, parts):
    total = None
    for g in range(5):
        row = (e * 5 + g) * 8
        term = diag_ref[row : row + 8, :] * parts[g * 4 + rp]
        total = term if total is None else total + term
    return total


def untile(tables_ref, base, tiles_of, count, tile_count, write):
    for t in range(tile_count):
        tables_ref[base + t * 8 : base + t * 8 + count, :] = tiles_of(slice(t * LANES, (t + 1) * LANES))
    for i in range(count):
        write(i, tables_ref[pl.ds(base + i, tile_count, stride=8), :])


def first_kernel(freq_ref, src_ref, near_in, jac_in, diag_in, flow_ref, weight_ref, *refs):
    freq = own_freq(freq_ref)
    scratch_ref, beside_ref = refs[10:]
    for h in range(2):
        near_ref, jac_ref, diag_ref, map_ref, part_ref = refs[h * 5 : h * 5 + 5]
        tables_ref = scratch_ref.at[h]
        start = h * near_ref.shape[0] // 6 * LANES

        def cells(lanes, start=start):
            return slice(start + lanes.start, start + lanes.stop)

        def write_near(j, rows, near_ref=near_ref):
            near_ref[j * 8 : j * 8 + 8, :] = rows.astype(jnp.int32)

        untile(tables_ref, 0, lambda lanes: near_in[:, cells(lanes)].astype(F32), 6, 8, write_near)
        for e in range(5):
            for g in range(5):

                def write_jac(j, rows, e=e, g=g, jac_ref=jac_ref):
                    at = ((j * 5 + e) * 5 + g) * 8
                    jac_ref[at : at + 8, :] = rows

                at = (6 + e * 5 + g) * 64
                untile(tables_ref, at, lambda lanes, e=e, g=g: jac_in[e, g, :, cells(lanes)].astype(F32), 6, 8, write_jac)

            def write_diag(g, rows, e=e, diag_ref=diag_ref):
                at = (e * 5 + g) * 8
                diag_ref[at : at + 8, :] = rows

            untile(tables_ref, (1 + e) * 64, lambda lanes, e=e: diag_in[e, :, cells(lanes)], 5, 8, write_diag)
        for q in range(2):
            weight = [None] * 20
            for g in range(5):
                weight[g * 4] = weight_ref[pl.ds(g * 32 + h * 16 + q, 8, stride=2), :]
            for e in range(5):
                row = (e * 2 + q) * 8
                map_ref[row : row + 8, :] = solve(diag_ref, e, 0, weight)
        coupling = local_coupling(h, freq, src_ref, near_ref, jac_ref, beside_ref.at[h])
        rest = [load_half(flow_ref, f, h) - coupling[f] for f in range(20)]
        for f in range(20):
            store_part(part_ref, f, solve(diag_ref, f // 4, f % 4, rest))


def wall_terms(freq, wall_of, map_ref):
    w = [wall_of(v) for v in range(8)]
    velocity = [-freq[0] * w[2], -freq[1] * w[3], freq[0] * w[0], freq[1] * w[1]]
    terms = []
    for e in range(5):
        m0 = map_ref[e * 16 : e * 16 + 8, :]
        m1 = map_ref[e * 16 + 8 : e * 16 + 16, :]
        terms += [m0 * velocity[rp] + m1 * w[4 + rp] for rp in range(4)]
    return terms


def last_kernel(freq_ref, src_ref, flow_ref, wall_ref, *refs):
    freq = own_freq(freq_ref)
    beside_ref = refs[10]
    for h in range(2):
        near_ref, jac_ref, diag_ref, map_ref = refs[h * 4 : h * 4 + 4]
        part_ref = refs[8 + h]
        terms = wall_terms(freq, lambda v: wall_ref[v * 16 + h * 8 : v * 16 + h * 8 + 8, :], map_ref)
        for f in range(20):
            store_part(part_ref, f, terms[f])
        coupling = local_coupling(h, freq, src_ref, near_ref, jac_ref, beside_ref.at[h])
        rest = [load_half(flow_ref, f, h) - coupling[f] for f in range(20)]
        for f in range(20):
            store_part(part_ref, f, load_part(part_ref, f) + solve(diag_ref, f // 4, f % 4, rest))


def ghost_kernel(g0, g1, g2, g3, *refs):
    ghosts = (g0, g1, g2, g3)
    out_ref, beside_ref = refs[8:]
    for h in range(2):
        near_ref, jac_ref, diag_ref, part_ref = refs[h * 4 : h * 4 + 4]
        coupling = couple(
            16, lambda f: [(ghosts[t // 2], f * 2 + t % 2) for t in range(8)], near_ref, jac_ref, beside_ref.at[h]
        )
        for f in range(20):
            store_half(out_ref, f, h, load_part(part_ref, f) - solve(diag_ref, f // 4, f % 4, coupling))


def wall_kernel(freq_ref, recv_ref, send_ref, pre_ref, map0, map1, it_ref, wall_ref, h0, h1, h2, h3, hl_ref):
    freq = own_freq(freq_ref)
    sources = recv_ref.shape[0] // 9
    iota_a = iota_rows(16)
    iota_b = iota_rows(LANES)
    for s in range(sources):
        store_split(hl_ref, s * 16, recv_ref[s * 9 : s * 9 + 8, :])
    total = None
    for c in range(0, sources, CHUNK):
        parts_a, parts_b = [], []
        for s in range(c, c + CHUNK):
            cell = bcast(recv_ref, s * 9 + 8, 16).astype(jnp.int32)
            mask = one_hot(iota_a, narrow(cell >> 7))
            parts_b.append(one_hot(iota_b, narrow(cell & 127)))
            parts_a.append([bcast(hl_ref, s * 16 + v, 16).astype(BF16) * mask for v in range(16)])
        total = add_to(total, parts_a, parts_b)
    wall = total[:LANES] + total[LANES:]
    wall_ref[...] = wall
    for h in range(2):
        terms = wall_terms(freq, lambda v: wall[v * 16 + h * 8 : v * 16 + h * 8 + 8], (map0, map1)[h])
        for f in range(20):
            store_half(it_ref, f, h, load_half(pre_ref, f, h) + terms[f])
    pick_rows(it_ref, send_ref, (h0, h1, h2, h3))


def to_rows(field):
    lead = field.shape[:-2]
    inner = field.reshape(*lead, 2, field.shape[-1] // LANES, LANES)
    return jnp.swapaxes(inner, -3, -2).reshape(-1, LANES)


def from_rows(rows, shape):
    inner = rows.reshape(*shape[:-2], shape[-1] // LANES, 2, LANES)
    return jnp.swapaxes(inner, -3, -2).reshape(shape)


NEAR_FACE = (0,)
NEAR_PICK = range(4)
NEAR_SEND = (0,)
ORDER = ((3, -2), (1, -1), (2, 2), (0, 1))


def exchange(blocks):
    ghosts = [None] * 4
    for k, by in ORDER:
        ghosts[k] = from_behind(blocks[k], "dom", by)
    return ghosts


def step(
    spline_blocks,
    modal_coeff,
    frequency,
    face_dest,
    face_cell,
    wall_weight,
    flow_rhs,
    previous,
    diag_inverse,
    off_jacobian,
    neighbor,
    send_list,
):
    dom = lax.axis_size("dom")
    halo = [((40, LANES), F32)] * 4
    part, small, field = ((160, LANES), F32), ((80, LANES), F32), ((320, LANES), F32)
    dest = face_dest.reshape(32, LANES)
    coef = modal_coeff.transpose(1, 2, 0).reshape(16, 64)
    operands = [pltpu.with_memory_space_constraint(x, pltpu.HBM) for x in (coef, spline_blocks)]
    faces = call(face_kernel, operands, [((4, 8, 1024), F32)], near_out=NEAR_FACE)[0]
    faces = lax.all_to_all(faces, "rep", split_axis=0, concat_axis=0, tiled=True)
    slot, freq = call(
        slot_kernel, (frequency, dest), [((32, LANES), jnp.int32), ((16, LANES), F32)], smem=1, near_out=(0, 1)
    )
    prev = to_rows(previous)
    rows_out = send_list.reshape(8, LANES)
    picked = call(pick_kernel, (prev, rows_out), halo, near_out=NEAR_PICK)
    ghosts = exchange(picked)
    send = call(
        dispatch_kernel,
        ((faces,), dest, (slot,), face_cell.reshape(32, LANES)),
        [((dom * 9, LANES), F32)],
        [pltpu.VMEM((512, LANES), F32)],
        near_out=NEAR_SEND,
    )[0]
    recv = lax.all_to_all(send.reshape(dom, 9, 1, LANES), "dom", split_axis=0, concat_axis=0, tiled=True)
    recv = recv.reshape(dom * 9, LANES)

    jac_in = off_jacobian.transpose(1, 2, 0, 3)
    flow, weight = to_rows(flow_rhs), to_rows(wall_weight)
    table = [((48, LANES), jnp.int32), ((1200, LANES), F32), ((200, LANES), F32), small, part]
    made = call(
        first_kernel,
        ((freq,), prev, neighbor, jac_in, diag_inverse, flow, weight),
        table * 2,
        [pltpu.VMEM((2, 31 * 64, LANES), F32), pltpu.VMEM((2, 960, LANES), F32)],
        near_out=range(10),
    )
    made = [(x,) for x in made]
    tables, maps, parts = made[0:3] + made[5:8], [made[3], made[8]], [made[4], made[9]]
    both_beside = [pltpu.VMEM((2, 960, LANES), F32)]

    def ghost_part(ghosts, parts, near_out):
        operands = (*[(g,) for g in ghosts], *tables[:3], parts[0], *tables[3:], parts[1])
        return call(ghost_kernel, operands, [field], both_beside, near_out=near_out)[0]

    pre = ghost_part(ghosts, parts, (0,))
    it, wall, *picked = call(
        wall_kernel,
        ((freq,), (recv,), (rows_out,), (pre,), *maps),
        [field, ((LANES, LANES), F32), *halo],
        [pltpu.VMEM((dom * 16, LANES), F32)],
        near_out=range(6),
    )
    ghosts = exchange(picked)
    parts = call(
        last_kernel,
        ((freq,), (it,), flow, (wall,), *tables[:3], maps[0], *tables[3:], maps[1]),
        [part, part],
        both_beside,
        near_out=(0, 1),
    )
    out = ghost_part(ghosts, [(p,) for p in parts], ())
    return from_rows(out, flow_rhs.shape)


def solution(mesh):
    return jax.shard_map(
        step,
        mesh=mesh,
        in_specs=(
            P(("dom", "rep"), None, None, None),
            P(),
            P(),
            P("dom", None),
            P("dom"),
            P(None, None, "dom"),
            P(None, None, "rep", "dom"),
            P(None, None, "rep", "dom"),
            P(None, None, "dom"),
            P(None, None, None, "dom"),
            P(None, "dom"),
            P(None, "dom"),
        ),
        out_specs=P(None, None, "rep", "dom"),
        check_vma=False,
    )
```
